32 devices in a mesh: tm: 8 (over z, x), slab: 4 (over y, core).
Axes of the slice: x: 2, y: 2, z: 4, core: 2. Of those that a mesh axis runs over, the one named last changes fastest.
Arguments:
- source: float32 [32, 256, 2048], P('tm', 'slab'), may hold values from -6 to 6
- guess: float32 [32, 256, 2048], P('tm', 'slab'), may hold values from -2.5 to 2.5
- field: float32 [32, 256, 2048], P('tm', 'slab'), may hold values from -2.5 to 2.5
Outputs:
- solution: float32 [32, 256, 2048], P('tm', 'slab')
- residual_new: float32 [32, 256, 2048], P('tm', 'slab')
- force: float32 [32, 256, 2048], P('tm', 'slab')
The draws below stay inside these ranges and needn't reach their ends.
All inputs are finite; a program needn't handle non-finite values.
Results may differ from the reference program's by a relative error of at most 0.000021.
Values sent between devices are 32-bit elements; how exact they have to be, the bound alone decides.
A program may use at most 64 MiB of HBM per device.

```python
import jax
import jax.numpy as jnp

COLS = 2048
NT = 32
NR = 256


def draw_source(key, part):
    ramp = (0.5 + jnp.arange(NT, dtype=jnp.float32) / (NT - 1))[:, None, None]
    base = jnp.clip(jax.random.normal(key, (NT, NR, COLS), jnp.float32), -4.0, 4.0)
    return base * ramp


def steps_of(own_key, shape, pieces, smallest, top_value):
    factor_of = 1.0
    for axis_at, parts in pieces:
        heights = jax.random.uniform(jax.random.fold_in(jax.random.fold_in(own_key, 6), axis_at), (parts,), jnp.float32, smallest / len(pieces), top_value / len(pieces))
        factor_of = factor_of * jnp.repeat(jnp.exp(heights), shape[axis_at] // parts).reshape((-1,) + (1,) * (len(shape) - 1 - axis_at))
    return factor_of


def noise(key, dims, width, reach, shards=(), kind=jnp.bfloat16):
    entries = width * jax.random.normal(key, dims, jnp.float32)
    if shards:
        entries = entries * steps_of(key, dims, shards, -0.22, 0.18)
    return jnp.clip(entries, -reach, reach).astype(kind)


def setup_inputs(seed: int = 0) -> dict:
    key_of = jax.random.split(jax.random.key(seed), 4)
    return {
        "source": draw_source(jax.random.fold_in(key_of[3], 71), 0),
        "guess": noise(key_of[1], (NT, NR, COLS), 0.3, 2.5, ((0, 8), (1, 4)), jnp.float32),
        "field": noise(key_of[2], (NT, NR, COLS), 0.3, 2.5, ((0, 8), (1, 4)), jnp.float32),
    }


HOP_WEIGHT = 0.125
BOSON_WEIGHT = 2.0


def hopping(padded, parity_even):
    center = padded[:, 1:-1, :]
    sideways = jnp.roll(center, 1, axis=2) + jnp.roll(center, -1, axis=2)
    vertical = jnp.where(parity_even, padded[:, 2:, :], padded[:, :-2, :])
    return center + HOP_WEIGHT * (sideways + vertical)


def reference(source, guess, field):
    slices_all, rows_all, columns_all = source.shape
    row_ids = jnp.arange(rows_all, dtype=jnp.int32)[:, None]
    column_ids = jnp.arange(columns_all, dtype=jnp.int32)[None, :]
    parity_even = ((row_ids + column_ids) % 2 == 0)[None]
    slice_ids = jnp.arange(slices_all, dtype=jnp.int32)
    sign_here = jnp.where(slice_ids == 0, -1.0, 1.0).astype(jnp.float32)[:, None, None]
    sign_after = jnp.where(slice_ids == slices_all - 1, -1.0, 1.0).astype(jnp.float32)[:, None, None]
    weights = jnp.exp(field)

    def kinetic(values):
        return hopping(jnp.pad(values, ((0, 0), (1, 1), (0, 0))), parity_even)

    def forward(values):
        hopped = kinetic(values)
        carried = weights * hopped
        image = values - sign_here * jnp.roll(carried, 1, axis=0)
        back = weights * sign_after * jnp.roll(image, -1, axis=0)
        return image, back, hopped

    def normal(values):
        image, back, hopped = forward(values)
        return image - kinetic(back)

    residual = source - normal(guess)
    norm_sq = jnp.sum(residual * residual)
    applied = normal(residual)
    curvature = jnp.sum(residual * applied)
    alpha = norm_sq / curvature
    solution = guess + alpha * residual
    residual_new = residual - alpha * applied
    image, back, hopped = forward(solution)
    force = BOSON_WEIGHT * field + 2.0 * back * hopped
    return solution, residual_new, force
```

```python
import functools

import jax
import jax.numpy as jnp
from jax import lax
from jax.experimental import pallas as pl
from jax.experimental.pallas import tpu as pltpu
from jax.sharding import PartitionSpec as P

HOP_WEIGHT = 0.125
BOSON_WEIGHT = 2.0
MESH = pl.DeviceIdType.MESH
TILE = 8
LANES = 128
LEAD = (2, 5)
PAST = 2


def kernel(
    nt, ns, L, R, C,
    src_h, g_h, f_h, sol_o, rn_o, fo_o,
    gp, bp, rp, qp, f, q, hg, hr, im, w, car, carr, c0, gN, cin, cN, rin, via,
    tot, acc, sums,
    near, far, lsem, hss, hrs, gss, grs, pss, prs, sss, srs, qss, qrs, vrs, fss, ass, ars,
):
    NB = R // TILE
    last = L - 1
    tm, sl = lax.axis_index("tm"), lax.axis_index("slab")
    nxt_t, prv_t = lax.rem(tm + 1, nt), lax.rem(tm + nt - 1, nt)
    up_s, dn_s = lax.rem(sl + ns - 1, ns), lax.rem(sl + 1, ns)
    has_up, has_dn = sl > 0, sl < ns - 1
    s_b = jnp.where(tm == 0, -1.0, 1.0).astype(jnp.float32)
    s_n = jnp.where(tm == nt - 1, -1.0, 1.0).astype(jnp.float32)
    odd = lax.rem(tm, 2) == 1
    even = jnp.logical_not(odd)
    pair_t = tm + 1 - 2 * lax.rem(tm, 2)
    hop_t = lax.rem(jnp.where(odd, tm + nt - 2, tm + 2), nt)
    me, n_dev = tm * ns + sl, nt * ns

    order = [last] + list(range(last))
    g_in = {t: pltpu.make_async_copy(g_h.at[t], gp.at[t, pl.ds(TILE, R)], lsem.at[0, t]) for t in order}
    f_in = {t: pltpu.make_async_copy(f_h.at[t], f.at[t], lsem.at[1, t]) for t in order}
    q_in = {t: pltpu.make_async_copy(src_h.at[t], q.at[t], lsem.at[2, t]) for t in order}
    for t in order:
        g_in[t].start()
        f_in[t].start()
    for t in range(L):
        q_in[t].start()

    barrier = pltpu.get_barrier_semaphore()

    def tell(k, c):
        pl.semaphore_signal(barrier, inc=1, device_id=(k // ns, lax.rem(k, ns)), device_id_type=MESH)
        return c

    lax.fori_loop(me + 1, n_dev, tell, 0)
    pl.when(me > 0)(lambda: pl.semaphore_wait(barrier, me))

    def remote(src, dst, send, recv, block):
        return pltpu.make_async_remote_copy(
            src_ref=src, dst_ref=dst, send_sem=send, recv_sem=recv,
            device_id=(block, sl), device_id_type=MESH)

    send_g = remote(g_h.at[0], gN, gss, grs, prv_t)

    def ready(sem, block, slab):
        pl.semaphore_signal(sem, inc=1, device_id=(block, slab), device_id_type=MESH)

    @pl.when(tm > 0)
    def _():
        ready(near.at[0], prv_t, sl)
        send_g.start()

    @pl.when(has_up)
    def _():
        ready(near.at[1], tm, up_s)

    wraps = nt > 2

    if wraps:
        @pl.when(tm == nt - 1)
        def _():
            ready(near.at[2], nxt_t, sl)

    def tell_far(k, c):
        block, slab = k // ns, lax.rem(k, ns)
        beside = jnp.logical_and(slab == sl, block == tm - 1)
        beside = jnp.logical_or(beside, jnp.logical_and(block == tm, slab == sl - 1))
        if wraps:
            beside = jnp.logical_or(beside, jnp.logical_and(slab == sl, tm - block == nt - 1))
        pl.when(jnp.logical_not(beside))(lambda: ready(far, block, slab))
        return c

    def halo(src, off, dst, lo, n, k, hold=None):
        ts = pl.ds(lo, n)
        up = pltpu.make_async_remote_copy(
            src_ref=src.at[ts, pl.ds(off, 1)], dst_ref=dst.at[ts, pl.ds(TILE + R, 1)],
            send_sem=hss.at[k, 0], recv_sem=hrs.at[k, 0],
            device_id=(tm, up_s), device_id_type=MESH)
        dn = pltpu.make_async_remote_copy(
            src_ref=src.at[ts, pl.ds(off + R - 1, 1)], dst_ref=dst.at[ts, pl.ds(TILE - 1, 1)],
            send_sem=hss.at[k, 1], recv_sem=hrs.at[k, 1],
            device_id=(tm, dn_s), device_id_type=MESH)

        @pl.when(has_up)
        def _():
            up.start()

        @pl.when(has_dn)
        def _():
            if hold is not None:
                pl.semaphore_wait(hold, 1)
            dn.start()

        def wait():
            @pl.when(has_up)
            def _():
                up.wait_send()
                dn.wait_recv()

            @pl.when(has_dn)
            def _():
                dn.wait_send()
                up.wait_recv()

        return wait

    x1 = halo(g_h, 0, gp, 0, L, 0, hold=near.at[1])

    lax.fori_loop(0, me, tell_far, 0)

    @pl.when(jnp.logical_not(has_up))
    def _():
        for p in (gp, bp, rp, qp):
            for t in range(L):
                p[t, 0:TILE, :] = jnp.zeros((TILE, C), jnp.float32)

    @pl.when(jnp.logical_not(has_dn))
    def _():
        for p in (gp, bp, rp, qp):
            for t in range(L):
                p[t, TILE + R:, :] = jnp.zeros((TILE, C), jnp.float32)

    sub = lax.broadcasted_iota(jnp.int32, (TILE, C), 0)
    parity = lax.rem(
        lax.broadcasted_iota(jnp.int32, (TILE, LANES), 0) + lax.broadcasted_iota(jnp.int32, (TILE, LANES), 1), 2)
    down = jnp.concatenate([parity] * (C // LANES), axis=1) == 0

    def rows(i, pad=0):
        return pl.ds(pl.multiple_of(i * TILE + pad, TILE), TILE)

    def hop(p, t, i):
        cur = p[t, rows(i, TILE), :]
        below = pltpu.roll(jnp.where(sub == 0, p[t, rows(i, 2 * TILE), :], cur), TILE - 1, 0)
        above = pltpu.roll(jnp.where(sub == TILE - 1, p[t, rows(i), :], cur), 1, 0)
        side = pltpu.roll(cur, 1, 1) + pltpu.roll(cur, C - 1, 1)
        return cur, cur + HOP_WEIGHT * (side + jnp.where(down, below, above))

    def fold(x):
        x = x * x
        parts = [x[:, k * LANES:(k + 1) * LANES] for k in range(C // LANES)]
        while len(parts) > 1:
            rest = parts[len(parts) // 2 * 2:]
            parts = [a + b for a, b in zip(parts[::2], parts[1::2])] + rest
        return parts[0]

    def each(n, body, init=0):
        return lax.fori_loop(0, n * NB, lambda j, c: body(j // NB, j % NB, c), init)

    zero = jnp.zeros((TILE, LANES), jnp.float32)
    tile = [pl.ds(i * TILE, TILE) for i in range(NB)]
    send_p = remote(car, cin, pss, prs, nxt_t)

    def send_s(i, to_pair):
        d = tile[i]
        return remote(c0.at[d], (via if to_pair else cN).at[d], sss.at[i], (vrs if to_pair else srs).at[i], pair_t)

    def send_q(i, to_pair):
        d = tile[i]
        return remote(carr.at[d], (via if to_pair else rin).at[d], qss.at[i], (vrs if to_pair else qrs).at[i], pair_t)

    def send_s_past(i):
        return remote(c0.at[tile[i]], cN.at[tile[i]], sss.at[i], srs.at[i], prv_t)

    def send_q_past(i):
        return remote(carr.at[tile[i]], rin.at[tile[i]], qss.at[i], qrs.at[i], nxt_t)

    cut = NB - PAST

    def hand_on(i, to_s):
        d = tile[i]
        return remote(via.at[d], (cN if to_s else rin).at[d], fss.at[i], (srs if to_s else qrs).at[i], hop_t)

    def pass_s(*chunks):
        def passing(some):
            for i in some:
                send_s(i, True).wait_recv()
                hand_on(i, True).start()

        passing([i for i in chunks if i < cut])
        if chunks[-1] >= cut:
            pl.when(tm < nt - 1)(lambda: passing(range(cut, NB)))

    def pass_q(*chunks):
        @pl.when(even)
        def _():
            for i in chunks:
                if i < cut:
                    send_q(i, True).wait_recv()
                    hand_on(i, False).start()

    def start_q(lo, hi):
        for flag, to_pair in ((even, False), (odd, True)):
            @pl.when(flag)
            def _():
                for i in range(LEAD[to_pair] if lo else 0, (cut if to_pair else NB) if hi else LEAD[to_pair]):
                    send_q(i, to_pair).start()

    g_in[last].wait()
    f_in[last].wait()
    x1()

    def body_a(_, i, c):
        cur, k = hop(gp, last, i)
        wv = jnp.exp(f[last, rows(i), :])
        w[last, rows(i), :] = wv
        hg[last, rows(i), :] = k
        car[rows(i), :] = wv * k
        return c

    each(1, body_a)

    @pl.when(tm < nt - 1)
    def _():
        pl.semaphore_wait(near.at[0], 1)

    send_p.start()

    for t in range(last):
        g_in[t].wait()
        f_in[t].wait()
    for t in range(L):
        q_in[t].wait()

    def body_b(base):
        def body(t, i, c):
            t = t + base
            cur, k = hop(gp, t, i)
            wv = jnp.exp(f[t, rows(i), :])
            w[t, rows(i), :] = wv
            hg[t, rows(i), :] = k
            image = gp[t + 1, rows(i, TILE), :] - wv * k
            q[t + 1, rows(i), :] = q[t + 1, rows(i), :] - image
            bp[t, rows(i, TILE), :] = wv * image
            return c
        return body

    each(1, body_b(0))
    x2c = halo(bp, TILE, bp, 0, 1, 7)

    @pl.when(tm == 0)
    def _():
        if wraps:
            pl.semaphore_wait(near.at[2], 1)
        send_g.start()

    each(last - 1, body_b(1))
    x2a = halo(bp, TILE, bp, 1, last - 1, 1)
    x2c()

    def body_c(_, i, c):
        cur, k = hop(bp, 0, i)
        c0[rows(i), :] = (q[0, rows(i), :] - gp[0, rows(i, TILE), :]) + k
        return c

    each(1, body_c)

    for flag, to_pair in ((even, True), (odd, False)):
        @pl.when(flag)
        def _():
            for i in range(cut):
                send_s(i, to_pair).start()

    for flag, to_pair in ((jnp.logical_and(even, tm != nt - 2), True), (odd, False)):
        @pl.when(flag)
        def _():
            for i in range(cut, NB):
                send_s(i, to_pair).start()

    def body_r(base):
        def body(t, i, c):
            t = t + base
            cur, k = hop(bp, t, i)
            r = q[t, rows(i), :] + k
            rp[t, rows(i, TILE), :] = r
            return c + fold(r)
        return body

    def body_f(base):
        def body(t, i, c):
            t = t + base
            cur, k = hop(rp, t, i)
            hr[t, rows(i), :] = k
            wv = w[t, rows(i), :]
            image = rp[t + 1, rows(i, TILE), :] - wv * k
            im[t + 1, rows(i), :] = image
            qp[t, rows(i, TILE), :] = wv * image
            return c + fold(image)
        return body

    def body_y(base):
        def body(t, i, c):
            t = t + base
            cur, k = hop(qp, t, i)
            im[t, rows(i), :] = im[t, rows(i), :] - k
            return c
        return body

    x2a()
    norm = each(last - 1, body_r(1), zero)
    x3c = halo(rp, TILE, rp, 1, last - 1, 8)
    x3c()
    curv = each(last - 2, body_f(1), zero)
    x4c = halo(qp, TILE, qp, 1, last - 2, 9)

    tot[0] = norm
    tot[1] = curv
    above = (n_dev - 1 - me) - (tm < nt - 1).astype(jnp.int32) - has_dn.astype(jnp.int32)
    if wraps:
        above = above - (tm == 0).astype(jnp.int32)
    pl.when(above > 0)(lambda: pl.semaphore_wait(far, above))

    def body_g(_, i, c):
        r = c0[rows(i), :] + s_b * cin[rows(i), :]
        rp[0, rows(i, TILE), :] = r
        return c + fold(r)

    def body_y0(_, i, c):
        cur, k = hop(qp, 0, i)
        im[0, rows(i), :] = rp[0, rows(i, TILE), :] - k
        return c

    def from_prev(passes):
        send_p.wait_recv()
        tot[0] += each(1, body_g, zero)
        x3b = halo(rp, TILE, rp, 0, 1, 4)
        passes(0)
        x3b()
        passes(1)
        tot[1] += each(1, body_f(0), zero)
        x4a = halo(qp, TILE, qp, 0, 1, 5)
        passes(2, 3)
        x4a()
        each(1, body_y0)
        passes(4)
        x4c()
        each(last - 2, body_y(1))
        passes(*range(5, NB))

    @pl.when(even)
    def _():
        from_prev(lambda *chunks: None)

    send_g.wait_recv()

    def body_d(_, i, c):
        image = s_n * gN[rows(i), :] - car[rows(i), :]
        bp[last, rows(i, TILE), :] = w[last, rows(i), :] * image
        return c

    each(1, body_d)
    x2b = halo(bp, TILE, bp, last, 1, 2)
    x2b()
    tot[0] += each(1, body_r(last), zero)
    x3a = halo(rp, TILE, rp, last, 1, 3)
    x3a()

    def body_e(_, i, c):
        cur, k = hop(rp, last, i)
        hr[last, rows(i), :] = k
        carr[rows(i), :] = w[last, rows(i), :] * k
        return c

    each(1, body_e)
    start_q(0, 0)
    tot[1] += each(1, body_f(last - 1), zero)
    x4d = halo(qp, TILE, qp, last - 1, 1, 10)

    @pl.when(tm == nt - 2)
    def _():
        send_s(cut - 1, True).wait_send()
        for i in range(cut, NB):
            send_s_past(i).start()

    x4d()
    each(1, body_y(last - 1))

    @pl.when(odd)
    def _():
        from_prev(pass_s)

    def body_h(_, i, c):
        carried = carr[rows(i), :]
        r_next = cN[rows(i), :] + s_n * car[rows(i), :]
        image = s_n * r_next - carried
        qp[last, rows(i, TILE), :] = w[last, rows(i), :] * image
        return c + fold(image)

    curv = tot[1]
    for i in range(NB):
        send_s(i, False).wait_recv()
        curv = body_h(0, i, curv)
    acc[0:1] = jnp.sum(tot[0], axis=0, keepdims=True)
    acc[1:2] = jnp.sum(curv, axis=0, keepdims=True)
    sums[me] = acc[...]

    def share(block, slab):
        pltpu.make_async_remote_copy(
            src_ref=acc, dst_ref=sums.at[me], send_sem=ass, recv_sem=ars,
            device_id=(block, slab), device_id_type=MESH).start()

    for k in range(ns):
        share(pair_t, lax.rem(sl + k, ns))
    for j in range(nt):
        block = lax.rem(tm + j, nt)
        if j == 1 or j == nt - 1:
            @pl.when(block != pair_t)
            def _():
                for k in range(ns):
                    share(block, lax.rem(sl + k, ns))
        else:
            for k in range(j == 0, ns):
                share(block, lax.rem(sl + k, ns))
    start_q(1, 1)
    x4b = halo(qp, TILE, qp, last, 1, 6)
    pass_q(0, 1)
    x4b()
    each(1, body_y(last))
    pass_q(*range(2, NB))

    @pl.when(odd)
    def _():
        send_q(cut - 1, True).wait_send()
        for i in range(cut, NB):
            send_q_past(i).start()

    others = pl.ds(0, n_dev - 1)
    shared = pltpu.make_async_remote_copy(
        src_ref=sums.at[others], dst_ref=sums.at[others], send_sem=ass, recv_sem=ars,
        device_id=(pair_t, sl), device_id_type=MESH)
    shared.wait_recv()
    total = sums[0]
    for k in range(1, n_dev):
        total = total + sums[k]
    ratio = jnp.full((TILE, LANES), jnp.sum(total[0:1])) / jnp.full((TILE, LANES), jnp.sum(total[1:2]))
    alpha = jnp.concatenate([ratio] * (C // LANES), axis=1)

    def body_s(t, i, c):
        sol_o[t, rows(i), :] = gp[t, rows(i, TILE), :] + alpha * rp[t, rows(i, TILE), :]
        back = bp[t, rows(i, TILE), :] + alpha * qp[t, rows(i, TILE), :]
        hopped = hg[t, rows(i), :] + alpha * hr[t, rows(i), :]
        fo_o[t, rows(i), :] = BOSON_WEIGHT * f[t, rows(i), :] + 2.0 * (back * hopped)
        return c

    def body_n(t, i, c):
        t = t + 1
        rn_o[t, rows(i), :] = rp[t, rows(i, TILE), :] - alpha * im[t, rows(i), :]
        return c

    each(L, body_s)
    each(last, body_n)
    for i, d in enumerate(tile):
        send_q(i, False).wait_recv()
        rn_o[0, d, :] = rp[0, pl.ds(TILE + i * TILE, TILE), :] - alpha * (im[0, d, :] - s_b * rin[d, :])
    send_g.wait_send()
    send_p.wait_send()
    shared.wait_send()
    for i in range(NB):
        if i != cut - 1:
            send_s(i, False).wait_send()
            send_q(i, False).wait_send()
        if i < cut:
            hand_on(i, True).wait_send()

    @pl.when(even)
    def _():
        send_q(cut - 1, False).wait_send()

    @pl.when(tm != nt - 2)
    def _():
        send_s(cut - 1, False).wait_send()

    @pl.when(jnp.logical_and(odd, tm < nt - 1))
    def _():
        for i in range(cut, NB):
            hand_on(i, True).wait_send()


def write_out(L, a, b, c, x, y, z, sem):
    copies = [pltpu.make_async_copy(src.at[t], dst.at[t], sem.at[j, t])
              for j, (src, dst) in enumerate(((a, x), (b, y), (c, z))) for t in range(L)]
    for copy in copies:
        copy.start()
    for copy in copies:
        copy.wait()


def on_device(source, guess, field):
    L, R, C = source.shape
    nt, ns = lax.axis_size("tm"), lax.axis_size("slab")
    NB = R // TILE
    f32 = jnp.float32
    padded = pltpu.VMEM((L, R + 2 * TILE, C), f32)
    whole = pltpu.VMEM((L, R, C), f32)
    one = pltpu.VMEM((R, C), f32)
    sems = lambda *shape: pltpu.SemaphoreType.DMA(shape)
    outs = pl.pallas_call(
        functools.partial(kernel, nt, ns, L, R, C),
        out_shape=[jax.ShapeDtypeStruct((L, R, C), f32)] * 3,
        in_specs=[pl.BlockSpec(memory_space=pltpu.HBM)] * 3,
        out_specs=[pl.BlockSpec(memory_space=pltpu.VMEM)] * 3,
        scratch_shapes=[padded] * 4 + [whole] * 6 + [one] * 8 + [
            pltpu.VMEM((2, TILE, LANES), f32),
            pltpu.VMEM((2, LANES), f32),
            pltpu.VMEM((nt * ns, 2, LANES), f32),
            pltpu.SemaphoreType.REGULAR((3,)), pltpu.SemaphoreType.REGULAR,
            sems(3, L), sems(11, 2), sems(11, 2), *[pltpu.SemaphoreType.DMA] * 4,
            *[sems(NB)] * 6, *[pltpu.SemaphoreType.DMA] * 2,
        ],
        compiler_params=pltpu.CompilerParams(
            collective_id=0, has_side_effects=True, vmem_limit_bytes=40 * 1024 * 1024),
    )(*(pltpu.with_memory_space_constraint(x, pltpu.HBM) for x in (source, guess, field)))
    return pl.pallas_call(
        functools.partial(write_out, L),
        out_shape=[jax.ShapeDtypeStruct((L, R, C), f32)] * 3,
        in_specs=[pl.BlockSpec(memory_space=pltpu.VMEM)] * 3,
        out_specs=[pl.BlockSpec(memory_space=pltpu.HBM)] * 3,
        scratch_shapes=[sems(3, L)],
        compiler_params=pltpu.CompilerParams(vmem_limit_bytes=8 * 1024 * 1024),
    )(*outs)


def solution(mesh):
    specs = (P("tm", "slab", None),) * 3
    return jax.shard_map(on_device, mesh=mesh, in_specs=specs, out_specs=specs, check_vma=False)
```

```python
import functools

import jax
import jax.numpy as jnp
from jax import lax
from jax.experimental import pallas as pl
from jax.experimental.pallas import tpu as pltpu
from jax.sharding import PartitionSpec as P

HOP_WEIGHT = 0.125
BOSON_WEIGHT = 2.0
MESH = pl.DeviceIdType.MESH
TILE = 8
LANES = 128
LEAD = (2, 5)
PAST = 2
EDGE_PAST = 3
C0_PAST = 1
EARLY = 2


def kernel(
    nt, ns, L, R, C,
    src_h, g_h, f_h, sol_o, rn_o, fo_o,
    gp, bp, rp, qp, f, q, hg, hr, im, w, car, carr, c0, gN, cin, cN, rin, via,
    tot, acc, sums,
    near, far, lsem, hss, hrs, gss, grs, pss, prs, sss, srs, qss, qrs, vrs, fss, ass, ars,
):
    NB = R // TILE
    last = L - 1
    tm, sl = lax.axis_index("tm"), lax.axis_index("slab")
    nxt_t, prv_t = lax.rem(tm + 1, nt), lax.rem(tm + nt - 1, nt)
    up_s, dn_s = lax.rem(sl + ns - 1, ns), lax.rem(sl + 1, ns)
    has_up, has_dn = sl > 0, sl < ns - 1
    s_b = jnp.where(tm == 0, -1.0, 1.0).astype(jnp.float32)
    s_n = jnp.where(tm == nt - 1, -1.0, 1.0).astype(jnp.float32)
    odd = lax.rem(tm, 2) == 1
    even = jnp.logical_not(odd)
    pair_t = tm + 1 - 2 * lax.rem(tm, 2)
    hop_t = lax.rem(jnp.where(odd, tm + nt - 2, tm + 2), nt)
    me, n_dev = tm * ns + sl, nt * ns

    order = [last] + list(range(last))
    g_in = {t: pltpu.make_async_copy(g_h.at[t], gp.at[t, pl.ds(TILE, R)], lsem.at[0, t]) for t in order}
    f_in = {t: pltpu.make_async_copy(f_h.at[t], f.at[t], lsem.at[1, t]) for t in order}
    q_in = {t: pltpu.make_async_copy(src_h.at[t], q.at[t], lsem.at[2, t]) for t in order}
    for t in order:
        g_in[t].start()
        f_in[t].start()
    for t in range(L):
        q_in[t].start()

    barrier = pltpu.get_barrier_semaphore()

    def tell(k, c):
        pl.semaphore_signal(barrier, inc=1, device_id=(k // ns, lax.rem(k, ns)), device_id_type=MESH)
        return c

    lax.fori_loop(me + 1, n_dev, tell, 0)
    pl.when(me > 0)(lambda: pl.semaphore_wait(barrier, me))

    def remote(src, dst, send, recv, block):
        return pltpu.make_async_remote_copy(
            src_ref=src, dst_ref=dst, send_sem=send, recv_sem=recv,
            device_id=(block, sl), device_id_type=MESH)

    send_g = remote(g_h.at[0], gN, gss, grs, prv_t)

    def ready(sem, block, slab):
        pl.semaphore_signal(sem, inc=1, device_id=(block, slab), device_id_type=MESH)

    @pl.when(tm > 0)
    def _():
        ready(near.at[0], prv_t, sl)
        send_g.start()

    @pl.when(has_up)
    def _():
        ready(near.at[1], tm, up_s)

    wraps = nt > 2

    if wraps:
        @pl.when(tm == nt - 1)
        def _():
            ready(near.at[2], nxt_t, sl)

    def tell_far(k, c):
        block, slab = k // ns, lax.rem(k, ns)
        beside = jnp.logical_and(slab == sl, block == tm - 1)
        beside = jnp.logical_or(beside, jnp.logical_and(block == tm, slab == sl - 1))
        if wraps:
            beside = jnp.logical_or(beside, jnp.logical_and(slab == sl, tm - block == nt - 1))
        pl.when(jnp.logical_not(beside))(lambda: ready(far, block, slab))
        return c

    def halo(src, off, dst, lo, n, k, hold=None):
        ts = pl.ds(lo, n)
        up = pltpu.make_async_remote_copy(
            src_ref=src.at[ts, pl.ds(off, 1)], dst_ref=dst.at[ts, pl.ds(TILE + R, 1)],
            send_sem=hss.at[k, 0], recv_sem=hrs.at[k, 0],
            device_id=(tm, up_s), device_id_type=MESH)
        dn = pltpu.make_async_remote_copy(
            src_ref=src.at[ts, pl.ds(off + R - 1, 1)], dst_ref=dst.at[ts, pl.ds(TILE - 1, 1)],
            send_sem=hss.at[k, 1], recv_sem=hrs.at[k, 1],
            device_id=(tm, dn_s), device_id_type=MESH)

        @pl.when(has_up)
        def _():
            up.start()

        @pl.when(has_dn)
        def _():
            if hold is not None:
                pl.semaphore_wait(hold, 1)
            dn.start()

        def wait():
            @pl.when(has_up)
            def _():
                up.wait_send()
                dn.wait_recv()

            @pl.when(has_dn)
            def _():
                dn.wait_send()
                up.wait_recv()

        return wait

    x1 = halo(g_h, 0, gp, 0, L, 0, hold=near.at[1])

    lax.fori_loop(0, me, tell_far, 0)

    @pl.when(jnp.logical_not(has_up))
    def _():
        for p in (gp, bp, rp, qp):
            for t in range(L):
                p[t, 0:TILE, :] = jnp.zeros((TILE, C), jnp.float32)

    @pl.when(jnp.logical_not(has_dn))
    def _():
        for p in (gp, bp, rp, qp):
            for t in range(L):
                p[t, TILE + R:, :] = jnp.zeros((TILE, C), jnp.float32)

    sub = lax.broadcasted_iota(jnp.int32, (TILE, C), 0)
    parity = lax.rem(
        lax.broadcasted_iota(jnp.int32, (TILE, LANES), 0) + lax.broadcasted_iota(jnp.int32, (TILE, LANES), 1), 2)
    down = jnp.concatenate([parity] * (C // LANES), axis=1) == 0

    def rows(i, pad=0):
        return pl.ds(pl.multiple_of(i * TILE + pad, TILE), TILE)

    def hop(p, t, i):
        cur = p[t, rows(i, TILE), :]
        below = pltpu.roll(jnp.where(sub == 0, p[t, rows(i, 2 * TILE), :], cur), TILE - 1, 0)
        above = pltpu.roll(jnp.where(sub == TILE - 1, p[t, rows(i), :], cur), 1, 0)
        side = pltpu.roll(cur, 1, 1) + pltpu.roll(cur, C - 1, 1)
        return cur, cur + HOP_WEIGHT * (side + jnp.where(down, below, above))

    def fold(x):
        x = x * x
        parts = [x[:, k * LANES:(k + 1) * LANES] for k in range(C // LANES)]
        while len(parts) > 1:
            rest = parts[len(parts) // 2 * 2:]
            parts = [a + b for a, b in zip(parts[::2], parts[1::2])] + rest
        return parts[0]

    def each(n, body, init=0):
        return lax.fori_loop(0, n * NB, lambda j, c: body(j // NB, j % NB, c), init)

    zero = jnp.zeros((TILE, LANES), jnp.float32)
    tile = [pl.ds(i * TILE, TILE) for i in range(NB)]
    send_p = remote(car, cin, pss, prs, nxt_t)

    def send_s(i, to_pair):
        d = tile[i]
        return remote(c0.at[d], (via if to_pair else cN).at[d], sss.at[i], (vrs if to_pair else srs).at[i], pair_t)

    def send_q(i, to_pair):
        d = tile[i]
        return remote(carr.at[d], (via if to_pair else rin).at[d], qss.at[i], (vrs if to_pair else qrs).at[i], pair_t)

    def send_s_past(i):
        return remote(c0.at[tile[i]], cN.at[tile[i]], sss.at[i], srs.at[i], prv_t)

    def send_q_past(i):
        return remote(carr.at[tile[i]], rin.at[tile[i]], qss.at[i], qrs.at[i], nxt_t)

    cut, end, c0_cut = NB - PAST, NB - EDGE_PAST, NB - C0_PAST
    inner = jnp.logical_and(tm > 1, tm < nt - 2)

    def hand_on(i, to_s):
        d = tile[i]
        return remote(via.at[d], (cN if to_s else rin).at[d], fss.at[i], (srs if to_s else qrs).at[i], hop_t)

    def pass_s(*chunks):
        def passing(some):
            for i in some:
                send_s(i, True).wait_recv()
                hand_on(i, True).start()

        passing([i for i in chunks if i < c0_cut])
        if chunks[-1] >= c0_cut:
            pl.when(tm < nt - 1)(lambda: passing(range(c0_cut, NB)))

    def pass_q(*chunks):
        def passing(i):
            send_q(i, True).wait_recv()
            hand_on(i, False).start()

        for i in chunks:
            if i < cut:
                pl.when(even if i < end else jnp.logical_and(even, inner))(lambda: passing(i))

    def first_of_q():
        @pl.when(even)
        def _():
            for i in range(LEAD[0]):
                send_q(i, False).start()

        @pl.when(odd)
        def _():
            for i in range(end):
                send_q(i, True).start()

        @pl.when(jnp.logical_and(odd, inner))
        def _():
            for i in range(end, LEAD[1]):
                send_q(i, True).start()

        @pl.when(tm == nt - 1)
        def _():
            for i in range(NB - EARLY, NB):
                send_q_past(i).start()

    def rest_of_q():
        @pl.when(even)
        def _():
            for i in range(LEAD[0], NB):
                send_q(i, False).start()

        @pl.when(jnp.logical_and(odd, inner))
        def _():
            for i in range(LEAD[1], cut):
                send_q(i, True).start()

    def end_of_q():
        @pl.when(jnp.logical_and(odd, inner))
        def _():
            send_q(cut - 1, True).wait_send()
            for i in range(cut, NB):
                send_q_past(i).start()

        @pl.when(jnp.logical_and(odd, jnp.logical_not(inner)))
        def _():
            for i in range(end, NB - EARLY):
                send_q_past(i).start()

        @pl.when(jnp.logical_and(tm == 1, tm < nt - 1))
        def _():
            for i in range(NB - EARLY, NB):
                send_q_past(i).start()

    g_in[last].wait()
    f_in[last].wait()
    x1()

    def body_a(_, i, c):
        cur, k = hop(gp, last, i)
        wv = jnp.exp(f[last, rows(i), :])
        w[last, rows(i), :] = wv
        hg[last, rows(i), :] = k
        car[rows(i), :] = wv * k
        return c

    each(1, body_a)

    @pl.when(tm < nt - 1)
    def _():
        pl.semaphore_wait(near.at[0], 1)

    send_p.start()

    for t in range(last):
        g_in[t].wait()
        f_in[t].wait()
    for t in range(L):
        q_in[t].wait()

    def body_b(base):
        def body(t, i, c):
            t = t + base
            cur, k = hop(gp, t, i)
            wv = jnp.exp(f[t, rows(i), :])
            w[t, rows(i), :] = wv
            hg[t, rows(i), :] = k
            image = gp[t + 1, rows(i, TILE), :] - wv * k
            q[t + 1, rows(i), :] = q[t + 1, rows(i), :] - image
            bp[t, rows(i, TILE), :] = wv * image
            return c
        return body

    each(1, body_b(0))
    x2c = halo(bp, TILE, bp, 0, 1, 7)

    @pl.when(tm == 0)
    def _():
        if wraps:
            pl.semaphore_wait(near.at[2], 1)
        send_g.start()

    each(last - 1, body_b(1))
    x2a = halo(bp, TILE, bp, 1, last - 1, 1)
    x2c()

    def body_c(_, i, c):
        cur, k = hop(bp, 0, i)
        c0[rows(i), :] = (q[0, rows(i), :] - gp[0, rows(i, TILE), :]) + k
        return c

    each(1, body_c)

    for flag, to_pair in ((even, True), (odd, False)):
        @pl.when(flag)
        def _():
            for i in range(c0_cut):
                send_s(i, to_pair).start()

    for flag, to_pair in ((jnp.logical_and(even, tm != nt - 2), True), (odd, False)):
        @pl.when(flag)
        def _():
            for i in range(c0_cut, NB):
                send_s(i, to_pair).start()

    def body_r(base):
        def body(t, i, c):
            t = t + base
            cur, k = hop(bp, t, i)
            r = q[t, rows(i), :] + k
            rp[t, rows(i, TILE), :] = r
            return c + fold(r)
        return body

    def body_f(base):
        def body(t, i, c):
            t = t + base
            cur, k = hop(rp, t, i)
            hr[t, rows(i), :] = k
            wv = w[t, rows(i), :]
            image = rp[t + 1, rows(i, TILE), :] - wv * k
            im[t + 1, rows(i), :] = image
            qp[t, rows(i, TILE), :] = wv * image
            return c + fold(image)
        return body

    def body_y(base):
        def body(t, i, c):
            t = t + base
            cur, k = hop(qp, t, i)
            im[t, rows(i), :] = im[t, rows(i), :] - k
            return c
        return body

    x2a()
    norm = each(last - 1, body_r(1), zero)
    x3c = halo(rp, TILE, rp, 1, last - 1, 8)
    x3c()
    curv = each(last - 2, body_f(1), zero)
    x4c = halo(qp, TILE, qp, 1, last - 2, 9)

    tot[0] = norm
    tot[1] = curv
    above = (n_dev - 1 - me) - (tm < nt - 1).astype(jnp.int32) - has_dn.astype(jnp.int32)
    if wraps:
        above = above - (tm == 0).astype(jnp.int32)
    pl.when(above > 0)(lambda: pl.semaphore_wait(far, above))

    def body_g(_, i, c):
        r = c0[rows(i), :] + s_b * cin[rows(i), :]
        rp[0, rows(i, TILE), :] = r
        return c + fold(r)

    def body_y0(_, i, c):
        cur, k = hop(qp, 0, i)
        im[0, rows(i), :] = rp[0, rows(i, TILE), :] - k
        return c

    def from_prev(passes):
        send_p.wait_recv()
        tot[0] += each(1, body_g, zero)
        x3b = halo(rp, TILE, rp, 0, 1, 4)
        passes(0)
        x3b()
        passes(1)
        tot[1] += each(1, body_f(0), zero)
        x4a = halo(qp, TILE, qp, 0, 1, 5)
        passes(2, 3)
        x4a()
        each(1, body_y0)
        passes(4)
        x4c()
        each(last - 2, body_y(1))
        passes(*range(5, NB))

    @pl.when(even)
    def _():
        from_prev(lambda *chunks: None)

    send_g.wait_recv()

    def body_d(_, i, c):
        image = s_n * gN[rows(i), :] - car[rows(i), :]
        bp[last, rows(i, TILE), :] = w[last, rows(i), :] * image
        return c

    each(1, body_d)
    x2b = halo(bp, TILE, bp, last, 1, 2)
    x2b()
    tot[0] += each(1, body_r(last), zero)
    x3a = halo(rp, TILE, rp, last, 1, 3)
    x3a()

    def body_e(_, i, c):
        cur, k = hop(rp, last, i)
        hr[last, rows(i), :] = k
        carr[rows(i), :] = w[last, rows(i), :] * k
        return c

    each(1, body_e)
    first_of_q()
    tot[1] += each(1, body_f(last - 1), zero)
    x4d = halo(qp, TILE, qp, last - 1, 1, 10)

    @pl.when(tm == nt - 2)
    def _():
        send_s(c0_cut - 1, True).wait_send()
        for i in range(c0_cut, NB):
            send_s_past(i).start()

    x4d()
    each(1, body_y(last - 1))

    @pl.when(odd)
    def _():
        from_prev(pass_s)

    def body_h(_, i, c):
        carried = carr[rows(i), :]
        r_next = cN[rows(i), :] + s_n * car[rows(i), :]
        image = s_n * r_next - carried
        qp[last, rows(i, TILE), :] = w[last, rows(i), :] * image
        return c + fold(image)

    curv = tot[1]
    for i in range(NB):
        send_s(i, False).wait_recv()
        curv = body_h(0, i, curv)
    acc[0:1] = jnp.sum(tot[0], axis=0, keepdims=True)
    acc[1:2] = jnp.sum(curv, axis=0, keepdims=True)
    sums[me] = acc[...]

    def share(block, slab):
        pltpu.make_async_remote_copy(
            src_ref=acc, dst_ref=sums.at[me], send_sem=ass, recv_sem=ars,
            device_id=(block, slab), device_id_type=MESH).start()

    for k in range(ns):
        share(pair_t, lax.rem(sl + k, ns))
    rest_of_q()
    for j in range(nt):
        block = lax.rem(tm + j, nt)
        if j == 1 or j == nt - 1:
            @pl.when(block != pair_t)
            def _():
                for k in range(ns):
                    share(block, lax.rem(sl + k, ns))
        else:
            for k in range(j == 0, ns):
                share(block, lax.rem(sl + k, ns))
    x4b = halo(qp, TILE, qp, last, 1, 6)
    pass_q(0, 1)
    x4b()
    each(1, body_y(last))
    pass_q(*range(2, NB))

    end_of_q()
    others = pl.ds(0, n_dev - 1)
    shared = pltpu.make_async_remote_copy(
        src_ref=sums.at[others], dst_ref=sums.at[others], send_sem=ass, recv_sem=ars,
        device_id=(pair_t, sl), device_id_type=MESH)
    shared.wait_recv()
    total = sums[0]
    for k in range(1, n_dev):
        total = total + sums[k]
    ratio = jnp.full((TILE, LANES), jnp.sum(total[0:1])) / jnp.full((TILE, LANES), jnp.sum(total[1:2]))
    alpha = jnp.concatenate([ratio] * (C // LANES), axis=1)

    def body_s(t, i, c):
        sol_o[t, rows(i), :] = gp[t, rows(i, TILE), :] + alpha * rp[t, rows(i, TILE), :]
        back = bp[t, rows(i, TILE), :] + alpha * qp[t, rows(i, TILE), :]
        hopped = hg[t, rows(i), :] + alpha * hr[t, rows(i), :]
        fo_o[t, rows(i), :] = BOSON_WEIGHT * f[t, rows(i), :] + 2.0 * (back * hopped)
        return c

    def body_n(t, i, c):
        t = t + 1
        rn_o[t, rows(i), :] = rp[t, rows(i, TILE), :] - alpha * im[t, rows(i), :]
        return c

    each(L, body_s)
    each(last, body_n)
    for i, d in enumerate(tile):
        send_q(i, False).wait_recv()
        rn_o[0, d, :] = rp[0, pl.ds(TILE + i * TILE, TILE), :] - alpha * (im[0, d, :] - s_b * rin[d, :])
    send_g.wait_send()
    send_p.wait_send()
    shared.wait_send()
    for i in range(NB):
        unless = [tm == nt - 2] if i == c0_cut - 1 else []
        pl.when(jnp.logical_not(unless[0]) if unless else me >= 0)(lambda: send_s(i, False).wait_send())
        pl.when(jnp.logical_not(odd & inner) if i == cut - 1 else me >= 0)(lambda: send_q(i, False).wait_send())
        gone = even & (inner & (i < cut) | (i < end)) | odd & ((tm < nt - 1) | (i < c0_cut))
        pl.when(gone)(lambda: hand_on(i, True).wait_send())


def write_out(L, a, b, c, x, y, z, sem):
    copies = [pltpu.make_async_copy(src.at[t], dst.at[t], sem.at[j, t])
              for j, (src, dst) in enumerate(((a, x), (b, y), (c, z))) for t in range(L)]
    for copy in copies:
        copy.start()
    for copy in copies:
        copy.wait()


def on_device(source, guess, field):
    L, R, C = source.shape
    nt, ns = lax.axis_size("tm"), lax.axis_size("slab")
    NB = R // TILE
    f32 = jnp.float32
    padded = pltpu.VMEM((L, R + 2 * TILE, C), f32)
    whole = pltpu.VMEM((L, R, C), f32)
    one = pltpu.VMEM((R, C), f32)
    sems = lambda *shape: pltpu.SemaphoreType.DMA(shape)
    outs = pl.pallas_call(
        functools.partial(kernel, nt, ns, L, R, C),
        out_shape=[jax.ShapeDtypeStruct((L, R, C), f32)] * 3,
        in_specs=[pl.BlockSpec(memory_space=pltpu.HBM)] * 3,
        out_specs=[pl.BlockSpec(memory_space=pltpu.VMEM)] * 3,
        scratch_shapes=[padded] * 4 + [whole] * 6 + [one] * 8 + [
            pltpu.VMEM((2, TILE, LANES), f32),
            pltpu.VMEM((2, LANES), f32),
            pltpu.VMEM((nt * ns, 2, LANES), f32),
            pltpu.SemaphoreType.REGULAR((3,)), pltpu.SemaphoreType.REGULAR,
            sems(3, L), sems(11, 2), sems(11, 2), *[pltpu.SemaphoreType.DMA] * 4,
            *[sems(NB)] * 6, *[pltpu.SemaphoreType.DMA] * 2,
        ],
        compiler_params=pltpu.CompilerParams(
            collective_id=0, has_side_effects=True, vmem_limit_bytes=40 * 1024 * 1024),
    )(*(pltpu.with_memory_space_constraint(x, pltpu.HBM) for x in (source, guess, field)))
    return pl.pallas_call(
        functools.partial(write_out, L),
        out_shape=[jax.ShapeDtypeStruct((L, R, C), f32)] * 3,
        in_specs=[pl.BlockSpec(memory_space=pltpu.VMEM)] * 3,
        out_specs=[pl.BlockSpec(memory_space=pltpu.HBM)] * 3,
        scratch_shapes=[sems(3, L)],
        compiler_params=pltpu.CompilerParams(vmem_limit_bytes=8 * 1024 * 1024),
    )(*outs)


def solution(mesh):
    specs = (P("tm", "slab", None),) * 3
    return jax.shard_map(on_device, mesh=mesh, in_specs=specs, out_specs=specs, check_vma=False)
```

```python
import functools

import jax
import jax.numpy as jnp
from jax import lax
from jax.experimental import pallas as pl
from jax.experimental.pallas import tpu as pltpu
from jax.sharding import PartitionSpec as P

HOP_WEIGHT = 0.125
BOSON_WEIGHT = 2.0
MESH = pl.DeviceIdType.MESH
TILE = 8
LANES = 128
LEAD = (2, 5)
PAST = 3
FIRST_PAST = 4
LAST_PAST = 4
C0_PAST = 1
EARLY = 2
PARTS = 1


def kernel(
    nt, ns, L, R, C,
    src_h, g_h, f_h,
    gp, bp, rp, qp, f, hg, hr, im, rin, al,
    q, w, car, carr, c0, gN, cin, cN, via,
    tot, acc, sums,
    near, far, lsem, hss, hrs, gss, grs, pss, prs, sss, srs, qss, qrs, vrs, fss, ass, ars,
):
    NB = R // TILE
    last = L - 1
    tm, sl = lax.axis_index("tm"), lax.axis_index("slab")
    nxt_t, prv_t = lax.rem(tm + 1, nt), lax.rem(tm + nt - 1, nt)
    up_s, dn_s = lax.rem(sl + ns - 1, ns), lax.rem(sl + 1, ns)
    has_up, has_dn = sl > 0, sl < ns - 1
    s_b = jnp.where(tm == 0, -1.0, 1.0).astype(jnp.float32)
    s_n = jnp.where(tm == nt - 1, -1.0, 1.0).astype(jnp.float32)
    odd = lax.rem(tm, 2) == 1
    even = jnp.logical_not(odd)
    pair_t = tm + 1 - 2 * lax.rem(tm, 2)
    hop_t = lax.rem(jnp.where(odd, tm + nt - 2, tm + 2), nt)
    me, n_dev = tm * ns + sl, nt * ns

    order = [last] + list(range(last))
    g_in = {t: pltpu.make_async_copy(g_h.at[t], gp.at[t, pl.ds(TILE, R)], lsem.at[0, t]) for t in order}
    f_in = {t: pltpu.make_async_copy(f_h.at[t], f.at[t], lsem.at[1, t]) for t in order}
    q_in = {t: pltpu.make_async_copy(src_h.at[t], q.at[t], lsem.at[2, t]) for t in order}
    for t in order:
        g_in[t].start()
        f_in[t].start()
    for t in range(L):
        q_in[t].start()

    barrier = pltpu.get_barrier_semaphore()

    def tell(k, c):
        pl.semaphore_signal(barrier, inc=1, device_id=(k // ns, lax.rem(k, ns)), device_id_type=MESH)
        return c

    lax.fori_loop(me + 1, n_dev, tell, 0)
    pl.when(me > 0)(lambda: pl.semaphore_wait(barrier, me))

    def remote(src, dst, send, recv, block):
        return pltpu.make_async_remote_copy(
            src_ref=src, dst_ref=dst, send_sem=send, recv_sem=recv,
            device_id=(block, sl), device_id_type=MESH)

    send_g = remote(g_h.at[0], gN, gss, grs, prv_t)

    def ready(sem, block, slab):
        pl.semaphore_signal(sem, inc=1, device_id=(block, slab), device_id_type=MESH)

    @pl.when(tm > 0)
    def _():
        ready(near.at[0], prv_t, sl)
        send_g.start()

    @pl.when(has_up)
    def _():
        ready(near.at[1], tm, up_s)

    wraps = nt > 2

    if wraps:
        @pl.when(tm == nt - 1)
        def _():
            ready(near.at[2], nxt_t, sl)

    def tell_far(k, c):
        block, slab = k // ns, lax.rem(k, ns)
        beside = jnp.logical_and(slab == sl, block == tm - 1)
        beside = jnp.logical_or(beside, jnp.logical_and(block == tm, slab == sl - 1))
        if wraps:
            beside = jnp.logical_or(beside, jnp.logical_and(slab == sl, tm - block == nt - 1))
        pl.when(jnp.logical_not(beside))(lambda: ready(far, block, slab))
        return c

    def halo(src, off, dst, lo, n, k, hold=None):
        ts = pl.ds(lo, n)
        up = pltpu.make_async_remote_copy(
            src_ref=src.at[ts, pl.ds(off, 1)], dst_ref=dst.at[ts, pl.ds(TILE + R, 1)],
            send_sem=hss.at[k, 0], recv_sem=hrs.at[k, 0],
            device_id=(tm, up_s), device_id_type=MESH)
        dn = pltpu.make_async_remote_copy(
            src_ref=src.at[ts, pl.ds(off + R - 1, 1)], dst_ref=dst.at[ts, pl.ds(TILE - 1, 1)],
            send_sem=hss.at[k, 1], recv_sem=hrs.at[k, 1],
            device_id=(tm, dn_s), device_id_type=MESH)

        @pl.when(has_up)
        def _():
            up.start()

        @pl.when(has_dn)
        def _():
            if hold is not None:
                pl.semaphore_wait(hold, 1)
            dn.start()

        def wait():
            @pl.when(has_up)
            def _():
                up.wait_send()
                dn.wait_recv()

            @pl.when(has_dn)
            def _():
                dn.wait_send()
                up.wait_recv()

        return wait

    x1 = halo(g_h, 0, gp, 0, L, 0, hold=near.at[1])

    lax.fori_loop(0, me, tell_far, 0)

    @pl.when(jnp.logical_not(has_up))
    def _():
        for p in (gp, bp, rp, qp):
            for t in range(L):
                p[t, 0:TILE, :] = jnp.zeros((TILE, C), jnp.float32)

    @pl.when(jnp.logical_not(has_dn))
    def _():
        for p in (gp, bp, rp, qp):
            for t in range(L):
                p[t, TILE + R:, :] = jnp.zeros((TILE, C), jnp.float32)

    sub = lax.broadcasted_iota(jnp.int32, (TILE, C), 0)
    parity = lax.rem(
        lax.broadcasted_iota(jnp.int32, (TILE, LANES), 0) + lax.broadcasted_iota(jnp.int32, (TILE, LANES), 1), 2)
    down = jnp.concatenate([parity] * (C // LANES), axis=1) == 0

    def rows(i, pad=0):
        return pl.ds(pl.multiple_of(i * TILE + pad, TILE), TILE)

    def hop(p, t, i):
        cur = p[t, rows(i, TILE), :]
        below = pltpu.roll(jnp.where(sub == 0, p[t, rows(i, 2 * TILE), :], cur), TILE - 1, 0)
        above = pltpu.roll(jnp.where(sub == TILE - 1, p[t, rows(i), :], cur), 1, 0)
        side = pltpu.roll(cur, 1, 1) + pltpu.roll(cur, C - 1, 1)
        return cur, cur + HOP_WEIGHT * (side + jnp.where(down, below, above))

    def fold(x):
        x = x * x
        parts = [x[:, k * LANES:(k + 1) * LANES] for k in range(C // LANES)]
        while len(parts) > 1:
            rest = parts[len(parts) // 2 * 2:]
            parts = [a + b for a, b in zip(parts[::2], parts[1::2])] + rest
        return parts[0]

    def each(n, body, init=0):
        return lax.fori_loop(0, n * NB, lambda j, c: body(j // NB, j % NB, c), init)

    zero = jnp.zeros((TILE, LANES), jnp.float32)
    tile = [pl.ds(i * TILE, TILE) for i in range(NB)]
    send_p = remote(car, cin, pss, prs, nxt_t)

    def send_s(i, to_pair):
        d = tile[i]
        return remote(c0.at[d], (via if to_pair else cN).at[d], sss.at[i], (vrs if to_pair else srs).at[i], pair_t)

    def send_q(i, to_pair):
        d = tile[i]
        return remote(carr.at[d], (via if to_pair else rin).at[d], qss.at[i], (vrs if to_pair else qrs).at[i], pair_t)

    def send_s_past(i):
        return remote(c0.at[tile[i]], cN.at[tile[i]], sss.at[i], srs.at[i], prv_t)

    def send_q_past(i):
        return remote(carr.at[tile[i]], rin.at[tile[i]], qss.at[i], qrs.at[i], nxt_t)

    cut, c0_cut = NB - PAST, NB - C0_PAST
    first_end, end = NB - FIRST_PAST, NB - LAST_PAST
    inner = jnp.logical_and(tm > 1, tm < nt - 2)

    def hand_on(i, to_s):
        d = tile[i]
        return remote(via.at[d], (cN if to_s else rin).at[d], fss.at[i], (srs if to_s else qrs).at[i], hop_t)

    def pass_s(*chunks):
        def passing(some):
            for i in some:
                send_s(i, True).wait_recv()
                hand_on(i, True).start()

        passing([i for i in chunks if i < c0_cut])
        if chunks[-1] >= c0_cut:
            pl.when(tm < nt - 1)(lambda: passing(range(c0_cut, NB)))

    def pass_q(*chunks):
        def passing(i):
            send_q(i, True).wait_recv()
            hand_on(i, False).start()

        for i in chunks:
            if i < cut:
                pl.when(even if i < end else jnp.logical_and(even, tm != nt - 2 if i < first_end else inner))(
                    lambda: passing(i))

    def first_of_q():
        @pl.when(even)
        def _():
            for i in range(LEAD[0]):
                send_q(i, False).start()

        @pl.when(odd)
        def _():
            for i in range(end):
                send_q(i, True).start()

        @pl.when(jnp.logical_and(odd, tm < nt - 1))
        def _():
            for i in range(end, first_end):
                send_q(i, True).start()

        @pl.when(jnp.logical_and(odd, inner))
        def _():
            for i in range(first_end, LEAD[1]):
                send_q(i, True).start()

        @pl.when(tm == nt - 1)
        def _():
            for i in range(NB - EARLY, NB):
                send_q_past(i).start()

    def rest_of_q():
        @pl.when(even)
        def _():
            for i in range(LEAD[0], NB):
                send_q(i, False).start()

        @pl.when(jnp.logical_and(odd, inner))
        def _():
            for i in range(max(LEAD[1], first_end), cut):
                send_q(i, True).start()

    def end_of_q():
        @pl.when(jnp.logical_and(odd, inner))
        def _():
            send_q(cut - 1, True).wait_send()
            for i in range(cut, NB):
                send_q_past(i).start()

    g_in[last].wait()
    f_in[last].wait()
    x1()

    def body_a(_, i, c):
        cur, k = hop(gp, last, i)
        wv = jnp.exp(f[last, rows(i), :])
        w[last, rows(i), :] = wv
        hg[last, rows(i), :] = k
        car[rows(i), :] = wv * k
        return c

    each(1, body_a)

    @pl.when(tm < nt - 1)
    def _():
        pl.semaphore_wait(near.at[0], 1)

    send_p.start()

    for t in range(last):
        g_in[t].wait()
        f_in[t].wait()
    for t in range(L):
        q_in[t].wait()

    def body_b(base):
        def body(t, i, c):
            t = t + base
            cur, k = hop(gp, t, i)
            wv = jnp.exp(f[t, rows(i), :])
            w[t, rows(i), :] = wv
            hg[t, rows(i), :] = k
            image = gp[t + 1, rows(i, TILE), :] - wv * k
            q[t + 1, rows(i), :] = q[t + 1, rows(i), :] - image
            bp[t, rows(i, TILE), :] = wv * image
            return c
        return body

    each(1, body_b(0))
    x2c = halo(bp, TILE, bp, 0, 1, 7)

    @pl.when(tm == 0)
    def _():
        if wraps:
            pl.semaphore_wait(near.at[2], 1)
        send_g.start()

    each(last - 1, body_b(1))
    x2a = halo(bp, TILE, bp, 1, last - 1, 1)
    x2c()

    def body_c(_, i, c):
        cur, k = hop(bp, 0, i)
        c0[rows(i), :] = (q[0, rows(i), :] - gp[0, rows(i, TILE), :]) + k
        return c

    each(1, body_c)

    for flag, to_pair in ((even, True), (odd, False)):
        @pl.when(flag)
        def _():
            for i in range(c0_cut):
                send_s(i, to_pair).start()

    for flag, to_pair in ((jnp.logical_and(even, tm != nt - 2), True), (odd, False)):
        @pl.when(flag)
        def _():
            for i in range(c0_cut, NB):
                send_s(i, to_pair).start()

    def body_r(base):
        def body(t, i, c):
            t = t + base
            cur, k = hop(bp, t, i)
            r = q[t, rows(i), :] + k
            rp[t, rows(i, TILE), :] = r
            return c + fold(r)
        return body

    def body_f(base):
        def body(t, i, c):
            t = t + base
            cur, k = hop(rp, t, i)
            hr[t, rows(i), :] = k
            wv = w[t, rows(i), :]
            image = rp[t + 1, rows(i, TILE), :] - wv * k
            im[t + 1, rows(i), :] = image
            qp[t, rows(i, TILE), :] = wv * image
            return c + fold(image)
        return body

    def body_y(base):
        def body(t, i, c):
            t = t + base
            cur, k = hop(qp, t, i)
            im[t, rows(i), :] = im[t, rows(i), :] - k
            return c
        return body

    x2a()
    norm = each(last - 1, body_r(1), zero)
    x3c = halo(rp, TILE, rp, 1, last - 1, 8)
    x3c()
    curv = each(last - 2, body_f(1), zero)
    x4c = halo(qp, TILE, qp, 1, last - 2, 9)

    tot[0] = norm
    tot[1] = curv
    above = (n_dev - 1 - me) - (tm < nt - 1).astype(jnp.int32) - has_dn.astype(jnp.int32)
    if wraps:
        above = above - (tm == 0).astype(jnp.int32)
    pl.when(above > 0)(lambda: pl.semaphore_wait(far, above))

    def body_g(_, i, c):
        r = c0[rows(i), :] + s_b * cin[rows(i), :]
        rp[0, rows(i, TILE), :] = r
        return c + fold(r)

    def body_y0(_, i, c):
        cur, k = hop(qp, 0, i)
        im[0, rows(i), :] = rp[0, rows(i, TILE), :] - k
        return c

    def from_prev(passes):
        send_p.wait_recv()
        tot[0] += each(1, body_g, zero)
        x3b = halo(rp, TILE, rp, 0, 1, 4)
        passes(0)
        x3b()
        passes(1)
        tot[1] += each(1, body_f(0), zero)
        x4a = halo(qp, TILE, qp, 0, 1, 5)
        passes(2, 3)
        x4a()
        each(1, body_y0)
        passes(4)
        x4c()
        each(last - 2, body_y(1))
        passes(*range(5, NB))

    @pl.when(even)
    def _():
        from_prev(lambda *chunks: None)

    send_g.wait_recv()

    def body_d(_, i, c):
        image = s_n * gN[rows(i), :] - car[rows(i), :]
        bp[last, rows(i, TILE), :] = w[last, rows(i), :] * image
        return c

    each(1, body_d)
    x2b = halo(bp, TILE, bp, last, 1, 2)
    x2b()
    tot[0] += each(1, body_r(last), zero)
    x3a = halo(rp, TILE, rp, last, 1, 3)
    x3a()

    def body_e(_, i, c):
        cur, k = hop(rp, last, i)
        hr[last, rows(i), :] = k
        carr[rows(i), :] = w[last, rows(i), :] * k
        return c

    each(1, body_e)
    first_of_q()
    tot[1] += each(1, body_f(last - 1), zero)
    x4d = halo(qp, TILE, qp, last - 1, 1, 10)

    @pl.when(tm == nt - 2)
    def _():
        send_s(c0_cut - 1, True).wait_send()
        for i in range(c0_cut, NB):
            send_s_past(i).start()

    x4d()
    each(1, body_y(last - 1))

    @pl.when(odd)
    def _():
        from_prev(pass_s)

    def body_h(_, i, c):
        carried = carr[rows(i), :]
        r_next = cN[rows(i), :] + s_n * car[rows(i), :]
        image = s_n * r_next - carried
        qp[last, rows(i, TILE), :] = w[last, rows(i), :] * image
        return c + fold(image)

    curv = tot[1]
    for i in range(NB):
        send_s(i, False).wait_recv()
        curv = body_h(0, i, curv)
    acc[0:1] = jnp.sum(tot[0], axis=0, keepdims=True)
    acc[1:2] = jnp.sum(curv, axis=0, keepdims=True)
    sums[me] = acc[...]

    def share(block, slab):
        pltpu.make_async_remote_copy(
            src_ref=acc, dst_ref=sums.at[me], send_sem=ass, recv_sem=ars,
            device_id=(block, slab), device_id_type=MESH).start()

    for k in range(ns):
        share(pair_t, lax.rem(sl + k, ns))
    rest_of_q()
    for j in range(nt):
        block = lax.rem(tm + j, nt)
        if j == 1 or j == nt - 1:
            @pl.when(block != pair_t)
            def _():
                for k in range(ns):
                    share(block, lax.rem(sl + k, ns))
        else:
            for k in range(j == 0, ns):
                share(block, lax.rem(sl + k, ns))
    @pl.when(jnp.logical_and(tm == 1, tm < nt - 1))
    def _():
        for i in range(first_end, NB):
            send_q_past(i).start()

    @pl.when(tm == nt - 1)
    def _():
        for i in range(end, NB - EARLY):
            send_q_past(i).start()

    x4b = halo(qp, TILE, qp, last, 1, 6)
    pass_q(0, 1)
    x4b()
    each(1, body_y(last))
    pass_q(*range(2, NB))

    end_of_q()
    others = pl.ds(0, n_dev - 1)
    shared = pltpu.make_async_remote_copy(
        src_ref=sums.at[others], dst_ref=sums.at[others], send_sem=ass, recv_sem=ars,
        device_id=(pair_t, sl), device_id_type=MESH)
    shared.wait_recv()
    total = sums[0]
    for k in range(1, n_dev):
        total = total + sums[k]
    ratio = jnp.full((TILE, LANES), jnp.sum(total[0:1])) / jnp.full((TILE, LANES), jnp.sum(total[1:2]))
    al[0] = ratio
    al[1] = jnp.full((TILE, LANES), s_b)
    for i in range(NB):
        send_q(i, False).wait_recv()
    send_g.wait_send()
    send_p.wait_send()
    shared.wait_send()
    for i in range(NB):
        unless = [tm == nt - 2] if i == c0_cut - 1 else []
        pl.when(jnp.logical_not(unless[0]) if unless else me >= 0)(lambda: send_s(i, False).wait_send())
        pl.when(jnp.logical_not(odd & inner) if i == cut - 1 else me >= 0)(lambda: send_q(i, False).wait_send())
        gone = even & (inner & (i < cut) | (tm != nt - 2) & (i < first_end) | (i < end)) | odd & ((tm < nt - 1) | (i < c0_cut))
        pl.when(gone)(lambda: hand_on(i, True).wait_send())


def finish(L, R, C, gp, bp, rp, qp, f, hg, hr, im, rin, al, sol_h, rn_h, fo_h, sol, rn, fo, sem):
    alpha, sign = (jnp.concatenate([al[k]] * (C // LANES), axis=1) for k in range(2))
    part = R // PARTS
    copies = []
    for t in list(range(1, L)) + [0]:
        for h in range(PARTS):
            def body(i, c):
                at = pl.ds(pl.multiple_of(h * part + i * TILE, TILE), TILE)
                padded = pl.ds(pl.multiple_of(h * part + i * TILE + TILE, TILE), TILE)
                r = rp[t, padded, :]
                sol[t, at, :] = gp[t, padded, :] + alpha * r
                back = bp[t, padded, :] + alpha * qp[t, padded, :]
                hopped = hg[t, at, :] + alpha * hr[t, at, :]
                fo[t, at, :] = BOSON_WEIGHT * f[t, at, :] + 2.0 * (back * hopped)
                applied = im[t, at, :] if t else im[0, at, :] - sign * rin[at, :]
                rn[t, at, :] = r - alpha * applied
                return c

            lax.fori_loop(0, part // TILE, body, 0)
            d = pl.ds(h * part, part)
            for j, (src, dst) in enumerate(((sol, sol_h), (rn, rn_h), (fo, fo_h))):
                copies.append(pltpu.make_async_copy(src.at[t, d], dst.at[t, d], sem.at[j, t, h]))
                copies[-1].start()
    for c in copies:
        c.wait()


def on_device(source, guess, field):
    L, R, C = source.shape
    nt, ns = lax.axis_size("tm"), lax.axis_size("slab")
    NB = R // TILE
    f32 = jnp.float32
    kept = [jax.ShapeDtypeStruct(shape, f32) for shape in (
        *[(L, R + 2 * TILE, C)] * 4, *[(L, R, C)] * 4, (R, C), (2, TILE, LANES))]
    whole = pltpu.VMEM((L, R, C), f32)
    one = pltpu.VMEM((R, C), f32)
    sems = lambda *shape: pltpu.SemaphoreType.DMA(shape)
    outs = pl.pallas_call(
        functools.partial(kernel, nt, ns, L, R, C),
        out_shape=kept,
        in_specs=[pl.BlockSpec(memory_space=pltpu.HBM)] * 3,
        out_specs=[pl.BlockSpec(memory_space=pltpu.VMEM)] * len(kept),
        scratch_shapes=[whole] * 2 + [one] * 7 + [
            pltpu.VMEM((2, TILE, LANES), f32),
            pltpu.VMEM((2, LANES), f32),
            pltpu.VMEM((nt * ns, 2, LANES), f32),
            pltpu.SemaphoreType.REGULAR((3,)), pltpu.SemaphoreType.REGULAR,
            sems(3, L), sems(11, 2), sems(11, 2), *[pltpu.SemaphoreType.DMA] * 4,
            *[sems(NB)] * 6, *[pltpu.SemaphoreType.DMA] * 2,
        ],
        compiler_params=pltpu.CompilerParams(
            collective_id=0, has_side_effects=True, vmem_limit_bytes=24 * 1024 * 1024),
    )(*(pltpu.with_memory_space_constraint(x, pltpu.HBM) for x in (source, guess, field)))
    return pl.pallas_call(
        functools.partial(finish, L, R, C),
        out_shape=[jax.ShapeDtypeStruct((L, R, C), f32)] * 3,
        in_specs=[pl.BlockSpec(memory_space=pltpu.VMEM)] * len(kept),
        out_specs=[pl.BlockSpec(memory_space=pltpu.HBM)] * 3,
        scratch_shapes=[whole] * 3 + [sems(3, L, PARTS)],
        compiler_params=pltpu.CompilerParams(vmem_limit_bytes=16 * 1024 * 1024),
    )(*outs)


def solution(mesh):
    specs = (P("tm", "slab", None),) * 3
    return jax.shard_map(on_device, mesh=mesh, in_specs=specs, out_specs=specs, check_vma=False)
```

```python
import functools

import jax
import jax.numpy as jnp
from jax import lax
from jax.experimental import pallas as pl
from jax.experimental.pallas import tpu as pltpu
from jax.sharding import PartitionSpec as P

HOP_WEIGHT = 0.125
BOSON_WEIGHT = 2.0
MESH = pl.DeviceIdType.MESH
TILE = 8
LANES = 128
LEAD = (2, 5)
PAST = 3
FIRST_PAST = 4
LAST_PAST = 4
C0_PAST = 1
EARLY = 2
PARTS = 2


def kernel(
    nt, ns, L, R, C,
    src_h, g_h, f_h,
    gp, bp, rp, qp, f, hg, hr, im, rin, al,
    q, w, car, carr, c0, gN, cin, cN, via,
    tot, acc, sums,
    near, far, lsem, hss, hrs, gss, grs, pss, prs, sss, srs, qss, qrs, vrs, fss, ass, ars,
):
    NB = R // TILE
    last = L - 1
    tm, sl = lax.axis_index("tm"), lax.axis_index("slab")
    nxt_t, prv_t = lax.rem(tm + 1, nt), lax.rem(tm + nt - 1, nt)
    up_s, dn_s = lax.rem(sl + ns - 1, ns), lax.rem(sl + 1, ns)
    has_up, has_dn = sl > 0, sl < ns - 1
    s_b = jnp.where(tm == 0, -1.0, 1.0).astype(jnp.float32)
    s_n = jnp.where(tm == nt - 1, -1.0, 1.0).astype(jnp.float32)
    odd = lax.rem(tm, 2) == 1
    even = jnp.logical_not(odd)
    pair_t = tm + 1 - 2 * lax.rem(tm, 2)
    hop_t = lax.rem(jnp.where(odd, tm + nt - 2, tm + 2), nt)
    me, n_dev = tm * ns + sl, nt * ns

    order = [last] + list(range(last))
    g_in = {t: pltpu.make_async_copy(g_h.at[t], gp.at[t, pl.ds(TILE, R)], lsem.at[0, t]) for t in order}
    f_in = {t: pltpu.make_async_copy(f_h.at[t], f.at[t], lsem.at[1, t]) for t in order}
    q_in = {t: pltpu.make_async_copy(src_h.at[t], q.at[t], lsem.at[2, t]) for t in order}
    for t in order:
        g_in[t].start()
        f_in[t].start()
    for t in range(L):
        q_in[t].start()

    barrier = pltpu.get_barrier_semaphore()

    def tell(k, c):
        pl.semaphore_signal(barrier, inc=1, device_id=(k // ns, lax.rem(k, ns)), device_id_type=MESH)
        return c

    lax.fori_loop(me + 1, n_dev, tell, 0)
    pl.when(me > 0)(lambda: pl.semaphore_wait(barrier, me))

    def remote(src, dst, send, recv, block):
        return pltpu.make_async_remote_copy(
            src_ref=src, dst_ref=dst, send_sem=send, recv_sem=recv,
            device_id=(block, sl), device_id_type=MESH)

    send_g = remote(g_h.at[0], gN, gss, grs, prv_t)

    def ready(sem, block, slab):
        pl.semaphore_signal(sem, inc=1, device_id=(block, slab), device_id_type=MESH)

    @pl.when(tm > 0)
    def _():
        ready(near.at[0], prv_t, sl)
        send_g.start()

    @pl.when(has_up)
    def _():
        ready(near.at[1], tm, up_s)

    wraps = nt > 2

    if wraps:
        @pl.when(tm == nt - 1)
        def _():
            ready(near.at[2], nxt_t, sl)

    def tell_far(k, c):
        block, slab = k // ns, lax.rem(k, ns)
        beside = jnp.logical_and(slab == sl, block == tm - 1)
        beside = jnp.logical_or(beside, jnp.logical_and(block == tm, slab == sl - 1))
        if wraps:
            beside = jnp.logical_or(beside, jnp.logical_and(slab == sl, tm - block == nt - 1))
        pl.when(jnp.logical_not(beside))(lambda: ready(far, block, slab))
        return c

    def halo(src, off, dst, lo, n, k, hold=None):
        ts = pl.ds(lo, n)
        up = pltpu.make_async_remote_copy(
            src_ref=src.at[ts, pl.ds(off, 1)], dst_ref=dst.at[ts, pl.ds(TILE + R, 1)],
            send_sem=hss.at[k, 0], recv_sem=hrs.at[k, 0],
            device_id=(tm, up_s), device_id_type=MESH)
        dn = pltpu.make_async_remote_copy(
            src_ref=src.at[ts, pl.ds(off + R - 1, 1)], dst_ref=dst.at[ts, pl.ds(TILE - 1, 1)],
            send_sem=hss.at[k, 1], recv_sem=hrs.at[k, 1],
            device_id=(tm, dn_s), device_id_type=MESH)

        @pl.when(has_up)
        def _():
            up.start()

        @pl.when(has_dn)
        def _():
            if hold is not None:
                pl.semaphore_wait(hold, 1)
            dn.start()

        def wait():
            @pl.when(has_up)
            def _():
                up.wait_send()
                dn.wait_recv()

            @pl.when(has_dn)
            def _():
                dn.wait_send()
                up.wait_recv()

        return wait

    x1 = halo(g_h, 0, gp, 0, L, 0, hold=near.at[1])

    lax.fori_loop(0, me, tell_far, 0)

    @pl.when(jnp.logical_not(has_up))
    def _():
        for p in (gp, bp, rp, qp):
            for t in range(L):
                p[t, 0:TILE, :] = jnp.zeros((TILE, C), jnp.float32)

    @pl.when(jnp.logical_not(has_dn))
    def _():
        for p in (gp, bp, rp, qp):
            for t in range(L):
                p[t, TILE + R:, :] = jnp.zeros((TILE, C), jnp.float32)

    sub = lax.broadcasted_iota(jnp.int32, (TILE, C), 0)
    parity = lax.rem(
        lax.broadcasted_iota(jnp.int32, (TILE, LANES), 0) + lax.broadcasted_iota(jnp.int32, (TILE, LANES), 1), 2)
    down = jnp.concatenate([parity] * (C // LANES), axis=1) == 0

    def rows(i, pad=0):
        return pl.ds(pl.multiple_of(i * TILE + pad, TILE), TILE)

    def hop(p, t, i):
        cur = p[t, rows(i, TILE), :]
        below = pltpu.roll(jnp.where(sub == 0, p[t, rows(i, 2 * TILE), :], cur), TILE - 1, 0)
        above = pltpu.roll(jnp.where(sub == TILE - 1, p[t, rows(i), :], cur), 1, 0)
        side = pltpu.roll(cur, 1, 1) + pltpu.roll(cur, C - 1, 1)
        return cur, cur + HOP_WEIGHT * (side + jnp.where(down, below, above))

    def fold(x):
        x = x * x
        parts = [x[:, k * LANES:(k + 1) * LANES] for k in range(C // LANES)]
        while len(parts) > 1:
            rest = parts[len(parts) // 2 * 2:]
            parts = [a + b for a, b in zip(parts[::2], parts[1::2])] + rest
        return parts[0]

    def each(n, body, init=0):
        return lax.fori_loop(0, n * NB, lambda j, c: body(j // NB, j % NB, c), init)

    zero = jnp.zeros((TILE, LANES), jnp.float32)
    tile = [pl.ds(i * TILE, TILE) for i in range(NB)]
    send_p = remote(car, cin, pss, prs, nxt_t)

    def send_s(i, to_pair):
        d = tile[i]
        return remote(c0.at[d], (via if to_pair else cN).at[d], sss.at[i], (vrs if to_pair else srs).at[i], pair_t)

    def send_q(i, to_pair):
        d = tile[i]
        return remote(carr.at[d], (via if to_pair else rin).at[d], qss.at[i], (vrs if to_pair else qrs).at[i], pair_t)

    def send_s_past(i):
        return remote(c0.at[tile[i]], cN.at[tile[i]], sss.at[i], srs.at[i], prv_t)

    def send_q_past(i):
        return remote(carr.at[tile[i]], rin.at[tile[i]], qss.at[i], qrs.at[i], nxt_t)

    cut, c0_cut = NB - PAST, NB - C0_PAST
    first_end, end = NB - FIRST_PAST, NB - LAST_PAST
    inner = jnp.logical_and(tm > 1, tm < nt - 2)

    def hand_on(i, to_s):
        d = tile[i]
        return remote(via.at[d], (cN if to_s else rin).at[d], fss.at[i], (srs if to_s else qrs).at[i], hop_t)

    def pass_s(*chunks):
        def passing(some):
            for i in some:
                send_s(i, True).wait_recv()
                hand_on(i, True).start()

        passing([i for i in chunks if i < c0_cut])
        if chunks[-1] >= c0_cut:
            pl.when(tm < nt - 1)(lambda: passing(range(c0_cut, NB)))

    def pass_q(*chunks):
        def passing(i):
            send_q(i, True).wait_recv()
            hand_on(i, False).start()

        for i in chunks:
            if i < cut:
                pl.when(even if i < end else jnp.logical_and(even, tm != nt - 2 if i < first_end else inner))(
                    lambda: passing(i))

    def first_of_q():
        @pl.when(even)
        def _():
            for i in range(LEAD[0]):
                send_q(i, False).start()

        @pl.when(odd)
        def _():
            for i in range(end):
                send_q(i, True).start()

        @pl.when(jnp.logical_and(odd, tm < nt - 1))
        def _():
            for i in range(end, first_end):
                send_q(i, True).start()

        @pl.when(jnp.logical_and(odd, inner))
        def _():
            for i in range(first_end, LEAD[1]):
                send_q(i, True).start()

        @pl.when(tm == nt - 1)
        def _():
            for i in range(NB - EARLY, NB):
                send_q_past(i).start()

    def rest_of_q():
        @pl.when(even)
        def _():
            for i in range(LEAD[0], NB):
                send_q(i, False).start()

        @pl.when(jnp.logical_and(odd, inner))
        def _():
            for i in range(max(LEAD[1], first_end), cut):
                send_q(i, True).start()

    def end_of_q():
        @pl.when(jnp.logical_and(odd, inner))
        def _():
            send_q(cut - 1, True).wait_send()
            for i in range(cut, NB):
                send_q_past(i).start()

    g_in[last].wait()
    f_in[last].wait()
    x1()

    def body_a(_, i, c):
        cur, k = hop(gp, last, i)
        wv = jnp.exp(f[last, rows(i), :])
        w[last, rows(i), :] = wv
        hg[last, rows(i), :] = k
        car[rows(i), :] = wv * k
        return c

    each(1, body_a)

    @pl.when(tm < nt - 1)
    def _():
        pl.semaphore_wait(near.at[0], 1)

    send_p.start()

    for t in range(last):
        g_in[t].wait()
        f_in[t].wait()
    for t in range(L):
        q_in[t].wait()

    def body_b(base):
        def body(t, i, c):
            t = t + base
            cur, k = hop(gp, t, i)
            wv = jnp.exp(f[t, rows(i), :])
            w[t, rows(i), :] = wv
            hg[t, rows(i), :] = k
            image = gp[t + 1, rows(i, TILE), :] - wv * k
            q[t + 1, rows(i), :] = q[t + 1, rows(i), :] - image
            bp[t, rows(i, TILE), :] = wv * image
            return c
        return body

    each(1, body_b(0))
    x2c = halo(bp, TILE, bp, 0, 1, 7)

    @pl.when(tm == 0)
    def _():
        if wraps:
            pl.semaphore_wait(near.at[2], 1)
        send_g.start()

    each(last - 1, body_b(1))
    x2a = halo(bp, TILE, bp, 1, last - 1, 1)
    x2c()

    def body_c(_, i, c):
        cur, k = hop(bp, 0, i)
        c0[rows(i), :] = (q[0, rows(i), :] - gp[0, rows(i, TILE), :]) + k
        return c

    each(1, body_c)

    for flag, to_pair in ((even, True), (odd, False)):
        @pl.when(flag)
        def _():
            for i in range(c0_cut):
                send_s(i, to_pair).start()

    for flag, to_pair in ((jnp.logical_and(even, tm != nt - 2), True), (odd, False)):
        @pl.when(flag)
        def _():
            for i in range(c0_cut, NB):
                send_s(i, to_pair).start()

    def body_r(base):
        def body(t, i, c):
            t = t + base
            cur, k = hop(bp, t, i)
            r = q[t, rows(i), :] + k
            rp[t, rows(i, TILE), :] = r
            return c + fold(r)
        return body

    def body_f(base):
        def body(t, i, c):
            t = t + base
            cur, k = hop(rp, t, i)
            hr[t, rows(i), :] = k
            wv = w[t, rows(i), :]
            image = rp[t + 1, rows(i, TILE), :] - wv * k
            im[t + 1, rows(i), :] = image
            qp[t, rows(i, TILE), :] = wv * image
            return c + fold(image)
        return body

    def body_y(base):
        def body(t, i, c):
            t = t + base
            cur, k = hop(qp, t, i)
            im[t, rows(i), :] = im[t, rows(i), :] - k
            return c
        return body

    x2a()
    norm = each(last - 1, body_r(1), zero)
    x3c = halo(rp, TILE, rp, 1, last - 1, 8)
    x3c()
    curv = each(last - 2, body_f(1), zero)
    x4c = halo(qp, TILE, qp, 1, last - 2, 9)

    tot[0] = norm
    tot[1] = curv
    above = (n_dev - 1 - me) - (tm < nt - 1).astype(jnp.int32) - has_dn.astype(jnp.int32)
    if wraps:
        above = above - (tm == 0).astype(jnp.int32)
    pl.when(above > 0)(lambda: pl.semaphore_wait(far, above))

    def body_g(_, i, c):
        r = c0[rows(i), :] + s_b * cin[rows(i), :]
        rp[0, rows(i, TILE), :] = r
        return c + fold(r)

    def body_y0(_, i, c):
        cur, k = hop(qp, 0, i)
        im[0, rows(i), :] = rp[0, rows(i, TILE), :] - k
        return c

    def from_prev(passes):
        send_p.wait_recv()
        tot[0] += each(1, body_g, zero)
        x3b = halo(rp, TILE, rp, 0, 1, 4)
        passes(0)
        x3b()
        passes(1)
        tot[1] += each(1, body_f(0), zero)
        x4a = halo(qp, TILE, qp, 0, 1, 5)
        passes(2, 3)
        x4a()
        each(1, body_y0)
        passes(4)
        x4c()
        each(last - 2, body_y(1))
        passes(*range(5, NB))

    @pl.when(even)
    def _():
        from_prev(lambda *chunks: None)

    send_g.wait_recv()

    def body_d(_, i, c):
        image = s_n * gN[rows(i), :] - car[rows(i), :]
        bp[last, rows(i, TILE), :] = w[last, rows(i), :] * image
        return c

    each(1, body_d)
    x2b = halo(bp, TILE, bp, last, 1, 2)
    x2b()
    tot[0] += each(1, body_r(last), zero)
    x3a = halo(rp, TILE, rp, last, 1, 3)
    x3a()

    def body_e(_, i, c):
        cur, k = hop(rp, last, i)
        hr[last, rows(i), :] = k
        carr[rows(i), :] = w[last, rows(i), :] * k
        return c

    each(1, body_e)
    first_of_q()
    tot[1] += each(1, body_f(last - 1), zero)
    x4d = halo(qp, TILE, qp, last - 1, 1, 10)

    @pl.when(tm == nt - 2)
    def _():
        send_s(c0_cut - 1, True).wait_send()
        for i in range(c0_cut, NB):
            send_s_past(i).start()

    x4d()
    each(1, body_y(last - 1))

    @pl.when(odd)
    def _():
        from_prev(pass_s)

    def body_h(_, i, c):
        carried = carr[rows(i), :]
        r_next = cN[rows(i), :] + s_n * car[rows(i), :]
        image = s_n * r_next - carried
        qp[last, rows(i, TILE), :] = w[last, rows(i), :] * image
        return c + fold(image)

    curv = tot[1]
    for i in range(NB):
        send_s(i, False).wait_recv()
        curv = body_h(0, i, curv)
    acc[0:1] = jnp.sum(tot[0], axis=0, keepdims=True)
    acc[1:2] = jnp.sum(curv, axis=0, keepdims=True)
    sums[me] = acc[...]

    def share(block, slab):
        pltpu.make_async_remote_copy(
            src_ref=acc, dst_ref=sums.at[me], send_sem=ass, recv_sem=ars,
            device_id=(block, slab), device_id_type=MESH).start()

    for k in range(ns):
        share(pair_t, lax.rem(sl + k, ns))
    rest_of_q()
    for j in range(nt):
        block = lax.rem(tm + j, nt)
        if j == 1 or j == nt - 1:
            @pl.when(block != pair_t)
            def _():
                for k in range(ns):
                    share(block, lax.rem(sl + k, ns))
        else:
            for k in range(j == 0, ns):
                share(block, lax.rem(sl + k, ns))
    @pl.when(jnp.logical_and(tm == 1, tm < nt - 1))
    def _():
        for i in range(first_end, NB):
            send_q_past(i).start()

    @pl.when(tm == nt - 1)
    def _():
        for i in range(end, NB - EARLY):
            send_q_past(i).start()

    x4b = halo(qp, TILE, qp, last, 1, 6)
    pass_q(0, 1)
    x4b()
    each(1, body_y(last))
    pass_q(*range(2, NB))

    end_of_q()
    others = pl.ds(0, n_dev - 1)
    shared = pltpu.make_async_remote_copy(
        src_ref=sums.at[others], dst_ref=sums.at[others], send_sem=ass, recv_sem=ars,
        device_id=(pair_t, sl), device_id_type=MESH)
    shared.wait_recv()
    total = sums[0]
    for k in range(1, n_dev):
        total = total + sums[k]
    both = jnp.sum(total, axis=1, keepdims=True)
    ratio = jnp.broadcast_to(both[0:1] / both[1:2], (TILE, LANES))
    al[0] = ratio
    al[1] = jnp.full((TILE, LANES), s_b)
    for i in range(NB):
        send_q(i, False).wait_recv()
    send_g.wait_send()
    send_p.wait_send()
    shared.wait_send()
    for i in range(NB):
        unless = [tm == nt - 2] if i == c0_cut - 1 else []
        pl.when(jnp.logical_not(unless[0]) if unless else me >= 0)(lambda: send_s(i, False).wait_send())
        pl.when(jnp.logical_not(odd & inner) if i == cut - 1 else me >= 0)(lambda: send_q(i, False).wait_send())
        gone = even & (inner & (i < cut) | (tm != nt - 2) & (i < first_end) | (i < end)) | odd & ((tm < nt - 1) | (i < c0_cut))
        pl.when(gone)(lambda: hand_on(i, True).wait_send())


def finish(L, R, C, gp, bp, rp, qp, f, hg, hr, im, rin, al, sol_h, rn_h, fo_h, sol, rn, fo, sem):
    alpha, sign = (jnp.concatenate([al[k]] * (C // LANES), axis=1) for k in range(2))
    part = R // PARTS
    copies = []
    for t in list(range(1, L)) + [0]:
        for h in range(PARTS):
            def body(i, c):
                at = pl.ds(pl.multiple_of(h * part + i * TILE, TILE), TILE)
                padded = pl.ds(pl.multiple_of(h * part + i * TILE + TILE, TILE), TILE)
                r = rp[t, padded, :]
                sol[t, at, :] = gp[t, padded, :] + alpha * r
                back = bp[t, padded, :] + alpha * qp[t, padded, :]
                hopped = hg[t, at, :] + alpha * hr[t, at, :]
                fo[t, at, :] = BOSON_WEIGHT * f[t, at, :] + 2.0 * (back * hopped)
                applied = im[t, at, :] if t else im[0, at, :] - sign * rin[at, :]
                rn[t, at, :] = r - alpha * applied
                return c

            lax.fori_loop(0, part // TILE, body, 0)
            d = pl.ds(h * part, part)
            for j, (src, dst) in enumerate(((sol, sol_h), (rn, rn_h), (fo, fo_h))):
                copies.append(pltpu.make_async_copy(src.at[t, d], dst.at[t, d], sem.at[j, t, h]))
                copies[-1].start()
    for c in copies:
        c.wait()


def on_device(source, guess, field):
    L, R, C = source.shape
    nt, ns = lax.axis_size("tm"), lax.axis_size("slab")
    NB = R // TILE
    f32 = jnp.float32
    kept = [jax.ShapeDtypeStruct(shape, f32) for shape in (
        *[(L, R + 2 * TILE, C)] * 4, *[(L, R, C)] * 4, (R, C), (2, TILE, LANES))]
    whole = pltpu.VMEM((L, R, C), f32)
    one = pltpu.VMEM((R, C), f32)
    sems = lambda *shape: pltpu.SemaphoreType.DMA(shape)
    outs = pl.pallas_call(
        functools.partial(kernel, nt, ns, L, R, C),
        out_shape=kept,
        in_specs=[pl.BlockSpec(memory_space=pltpu.HBM)] * 3,
        out_specs=[pl.BlockSpec(memory_space=pltpu.VMEM)] * len(kept),
        scratch_shapes=[whole] * 2 + [one] * 7 + [
            pltpu.VMEM((2, TILE, LANES), f32),
            pltpu.VMEM((2, LANES), f32),
            pltpu.VMEM((nt * ns, 2, LANES), f32),
            pltpu.SemaphoreType.REGULAR((3,)), pltpu.SemaphoreType.REGULAR,
            sems(3, L), sems(11, 2), sems(11, 2), *[pltpu.SemaphoreType.DMA] * 4,
            *[sems(NB)] * 6, *[pltpu.SemaphoreType.DMA] * 2,
        ],
        compiler_params=pltpu.CompilerParams(
            collective_id=0, has_side_effects=True, vmem_limit_bytes=24 * 1024 * 1024),
    )(*(pltpu.with_memory_space_constraint(x, pltpu.HBM) for x in (source, guess, field)))
    return pl.pallas_call(
        functools.partial(finish, L, R, C),
        out_shape=[jax.ShapeDtypeStruct((L, R, C), f32)] * 3,
        in_specs=[pl.BlockSpec(memory_space=pltpu.VMEM)] * len(kept),
        out_specs=[pl.BlockSpec(memory_space=pltpu.HBM)] * 3,
        scratch_shapes=[whole] * 3 + [sems(3, L, PARTS)],
        compiler_params=pltpu.CompilerParams(vmem_limit_bytes=16 * 1024 * 1024),
    )(*outs)


def solution(mesh):
    specs = (P("tm", "slab", None),) * 3
    return jax.shard_map(on_device, mesh=mesh, in_specs=specs, out_specs=specs, check_vma=False)
```
